256 devices in a mesh: ctx: 16 (over z_hi, y, core), exp: 16 (over z_lo, x).
Axes of the slice: x: 4, y: 4, z: 8 (z_hi: 2, z_lo: 4; z = z_hi * 4 + z_lo), core: 2. Of those that a mesh axis runs over, the one named last changes fastest.
Arguments:
- residual: bfloat16 [16, 2048, 7168], P('exp', 'ctx'), may hold values from -6 to 6
- queries: bfloat16 [16, 2048, 1024], P('exp', 'ctx'), may hold values from -64 to 64
- latent: bfloat16 [16, 2048, 512], P('exp', 'ctx'), may hold values from -6 to 6
- out_proj: bfloat16 [1024, 7168], P('ctx'), may hold values from -0.5 to 0.5
- up_weight: bfloat16 [16, 7168, 1024], P('exp', 'ctx'), may hold values from -0.0625 to 0.0625
- down_weight: bfloat16 [16, 1024, 7168], P('exp', None, 'ctx'), may hold values from -0.1875 to 0.1875
- cotangent: bfloat16 [16, 2048, 7168], P('exp', 'ctx'), may hold values from -6 to 6
- routes: int32 [16, 2048, 8], P('exp', 'ctx'), may hold values from 0 to 255, as said below
- gate_values: float32 [16, 2048, 8], P('exp', 'ctx'), may hold values from 0.2 to 1
- documents: int32 [16, 16], P('exp'), may hold values from 0 to 2, never falling along the last dimension, each value on 1 to 8 neighbouring positions
Outputs:
- layer_out: bfloat16 [16, 2048, 7168], P('exp', 'ctx')
- input_grad: bfloat16 [16, 2048, 7168], P('exp', 'ctx')
- up_grad: bfloat16 [16, 7168, 1024], P('exp', 'ctx')
- down_grad: bfloat16 [16, 1024, 7168], P('exp', None, 'ctx')
The draws below stay inside these ranges and needn't reach their ends.
Inputs may be any that keep to these rules, and one draw needn't show every extreme that they name: Each token's 8 experts differ. Within one block of 128 consecutive tokens of a sequence at most 4 routes name one expert below 16, and in every draw some expert below 16 is named by exactly 4 routes of every such block. `documents`: document numbers never fall along a sequence; a document covers 1 to 8 consecutive blocks, and one covers exactly 8.
All inputs are finite; a program needn't handle non-finite values.
Results may differ from the reference program's by a relative error of at most 0.025.
Values may be sent and summed in bfloat16 or wider, within the bound.
No kernel may reach another device: no remote copies, remote signals or barrier semaphores. Data moves between devices by JAX's collectives and lax.ppermute only.
A program may use at most 128 MiB of HBM per device.

```python
import math
import jax
import jax.numpy as jnp
import numpy as np
from jax import lax

D = 7168
FF = 1024
ALL_EXPERTS = 256
TOP = 8
LAT = 512
HEADS = 2
CAP = 4
BLOCK = 128
DOCS = 3
TOK_DEV = 128
LEN = 2048
SEQS = 16
EXPERTS = 16
NBLK = 16
DOC_MAX = 8


def latent_pair(key):
    folded = jax.random.fold_in(key, 7)
    key_lat, key_query = jax.random.split(folded, 2)
    latent_draw = jax.random.normal(key_lat, (SEQS, LEN, LAT), jnp.float32)
    query_draw = jax.random.normal(key_query, (SEQS, LEN, HEADS, LAT), jnp.float32)
    latent_draw = jnp.clip(latent_draw, -6.0, 6.0)
    query_draw = jnp.clip(query_draw, -64.0, 64.0)
    return (query_draw.reshape(SEQS, LEN, HEADS * LAT), latent_draw)


def draw_queries(key, part):
    return latent_pair(key)[0].astype(jnp.bfloat16)


def draw_latent(key, part):
    return latent_pair(key)[1].astype(jnp.bfloat16)


def draw_routes(key, part):
    folded = jax.random.fold_in(key, 3)
    key_count, key_hot, key_perm, key_fill, key_roll = jax.random.split(folded, 5)
    blocks = SEQS * LEN // TOK_DEV
    counts = jax.random.randint(key_count, (blocks, EXPERTS), 0, CAP + 1)
    hottest = jax.random.randint(key_hot, (), 0, EXPERTS)
    experts_iota = jnp.arange(EXPERTS)
    counts = jnp.where(experts_iota[None, :] == hottest, CAP, counts)

    def shuffle_one(subkey):
        return jax.random.permutation(subkey, TOK_DEV)
    orders = jax.vmap(shuffle_one)(jax.random.split(key_perm, blocks))
    places = jnp.argsort(orders, axis=-1, stable=True)
    offset = (places[:, :, None] - experts_iota[None, None, :] * CAP) % TOK_DEV
    member = offset < counts[:, None, :]
    ranked = jnp.argsort(jnp.where(member, experts_iota, EXPERTS + experts_iota), axis=-1, stable=True)[:, :, :TOP]
    member_count = jnp.sum(member.astype(jnp.int32), axis=-1)
    spare = ALL_EXPERTS - EXPERTS
    start_at = jax.random.randint(key_fill, (blocks, TOK_DEV, 1), 0, spare)
    slots_iota = jnp.arange(TOP)
    filler = EXPERTS + (start_at + slots_iota * (spare // TOP)) % spare
    chosen = jnp.where(slots_iota[None, None, :] < member_count[:, :, None], ranked, filler)
    rotation = jax.random.randint(key_roll, (blocks, TOK_DEV, 1), 0, TOP)
    chosen = jnp.take_along_axis(chosen, (slots_iota[None, None, :] + rotation) % TOP, axis=-1)
    return chosen.reshape(SEQS, LEN, TOP).astype(jnp.int32)


def levels(key, shape, cuts, smallest, high):
    def one(axis_at, parts):
        draws = jax.random.uniform(jax.random.fold_in(jax.random.fold_in(key, 6), axis_at), (parts,), jnp.float32, smallest / len(cuts), high / len(cuts))
        return jnp.repeat(jnp.exp(draws), shape[axis_at] // parts).reshape((-1,) + (1,) * (len(shape) - axis_at - 1))

    gain = one(*cuts[0])
    for cut in cuts[1:]:
        gain = gain * one(*cut)
    return gain


def profile(amount, total, most, lean):
    portions = [(1 << 20) // math.isqrt(standing ** lean) + 1 for standing in range(2, amount + 1)]
    spare, given = total - most - (amount - 1), [1] * (amount - 1)
    while spare > 0:
        candidates = [i for i in range(amount - 1) if given[i] < most]
        mass, budget = sum([portions[i] for i in candidates]), spare
        for i in candidates:
            more = min(most - given[i], max(1, budget * portions[i] // mass), spare)
            given[i] = given[i] + more
            spare = spare - more
    return np.array([most] + given)


def uneven_parts(key, amount, total, bound, skew):
    if amount == 2:
        one = jax.random.randint(key, (), max(1, total - bound), min(bound, total - 1) + 1)
        return jnp.stack([one, total - one])
    tallies = jnp.asarray(profile(amount, total, bound, skew), jnp.int32)
    twos = (amount - 1) // 2
    giver, receiver = tallies[1:1 + 2 * twos:2], tallies[2:2 + 2 * twos:2]
    slack = jnp.minimum(giver - 1, bound - receiver)
    moved = jax.random.randint(jax.random.fold_in(key, 1), (twos,), 0, 1 << 20) % (slack + 1)
    tallies = tallies.at[1:1 + 2 * twos:2].set(giver - moved).at[2:2 + 2 * twos:2].set(receiver + moved)
    return tallies[jax.random.permutation(jax.random.fold_in(key, 2), amount)]


def bell_draw(key, dims, scale, most, shards=(), kind=jnp.bfloat16):
    entries = scale * jax.random.normal(key, dims, jnp.float32)
    if shards:
        entries = entries * levels(key, dims, shards, -0.22, 0.18)
    return jnp.clip(entries, -most, most).astype(kind)


def setup_inputs(seed: int = 0) -> dict:
    arg_keys = jax.random.split(jax.random.key(seed), 11)
    return {
        "residual": bell_draw(arg_keys[0], (SEQS, LEN, D), 1.0, 6.0, ((0, 16), (1, 16))),
        "queries": draw_queries(jax.random.fold_in(arg_keys[10], 71), 0),
        "latent": draw_latent(jax.random.fold_in(arg_keys[10], 71), 0),
        "out_proj": bell_draw(arg_keys[3], (HEADS * LAT, D), (HEADS * LAT // 8) ** -0.5, 0.5, ((0, 16),)),
        "up_weight": bell_draw(arg_keys[4], (EXPERTS, D, FF), D ** -0.5, 0.0625, ((0, 16), (1, 16))),
        "down_weight": bell_draw(arg_keys[5], (EXPERTS, FF, D), FF ** -0.5, 0.1875, ((0, 16), (2, 16))),
        "cotangent": bell_draw(arg_keys[6], (SEQS, LEN, D), 1.0, 6.0, ((0, 16), (1, 16))),
        "routes": draw_routes(jax.random.fold_in(arg_keys[10], 71), 0),
        "gate_values": jnp.clip(0.2 + 0.8 * jax.random.uniform(arg_keys[8], (SEQS, LEN, TOP), jnp.float32) ** levels(arg_keys[8], (SEQS, LEN, TOP), ((0, 16), (1, 16)), -0.2, 0.2), 0.2, 1.0),
        "documents": jax.vmap(lambda own: jnp.searchsorted(jnp.cumsum(uneven_parts(own, DOCS, NBLK, DOC_MAX, 2)), jnp.arange(NBLK), side="right"))(jax.random.split(arg_keys[9], SEQS)).reshape((SEQS, NBLK)).astype(jnp.int32),
    }


def silu_grad(values_in):
    sigmoid_of = jax.nn.sigmoid(values_in)
    return sigmoid_of * (1.0 + values_in * (1.0 - sigmoid_of))

def slot_tables(route_rows, gate_rows):
    experts = jnp.arange(EXPERTS, dtype=jnp.int32)
    onehot = (route_rows[:, :, None] == experts[None, None, :]).astype(jnp.int32)
    flat_hits = onehot.reshape(-1, EXPERTS)
    before = jnp.cumsum(flat_hits, axis=0) - flat_hits
    rank_in = lax.optimization_barrier(jnp.sum(before * flat_hits, axis=1)).reshape(route_rows.shape)
    valid = route_rows < EXPERTS
    slot_index = jnp.where(valid, route_rows * CAP + rank_in, -1)
    slots_all = jnp.arange(EXPERTS * CAP, dtype=jnp.int32)
    slot_hits = slot_index[None, :, :] == slots_all[:, None, None]
    picker = lax.optimization_barrier(jnp.sum(slot_hits.astype(jnp.float32), axis=2))
    weigher = lax.optimization_barrier(jnp.sum(jnp.where(slot_hits, gate_rows[None, :, :], 0.0), axis=2))
    return (picker, weigher)

def reference(residual, queries, latent, out_proj, up_weight, down_weight, cotangent, routes, gate_values, documents):
    inv_root = 1.0 / math.sqrt(LAT)

    def attend(inputs):
        query_seq, latent_seq, doc_seq = inputs
        query_f = query_seq.astype(jnp.float32).reshape(LEN, HEADS, LAT)
        latent_f = latent_seq.astype(jnp.float32)
        scores = jnp.einsum('ihk,jk->hij', query_f, latent_f) * inv_root
        positions = jnp.arange(LEN, dtype=jnp.int32)
        owner_doc = doc_seq[positions // BLOCK]
        allowed = (owner_doc[None, :] == owner_doc[:, None]) & (positions[None, :] <= positions[:, None])
        scores = jnp.where(allowed[None, :, :], scores, -jnp.inf)
        largest = lax.optimization_barrier(jnp.max(scores, axis=2, keepdims=True))
        exponent = jnp.where(allowed[None, :, :], jnp.exp(scores - largest), 0.0)
        total_sum = lax.optimization_barrier(jnp.sum(exponent, axis=2))
        rounded = lax.optimization_barrier(exponent.astype(jnp.bfloat16)).astype(jnp.float32)
        mixed_rows = jnp.einsum('hij,jk->ihk', rounded, latent_f) / jnp.transpose(total_sum)[:, :, None]
        return mixed_rows.astype(jnp.bfloat16).reshape(LEN, HEADS * LAT)
    heads_out = lax.map(attend, (queries, latent, documents))
    projected = jnp.dot(heads_out.reshape(SEQS * LEN, HEADS * LAT), out_proj, preferred_element_type=jnp.float32)
    hidden_in = (residual.reshape(SEQS * LEN, D).astype(jnp.float32) + projected).astype(jnp.bfloat16)
    blocks = SEQS * LEN // TOK_DEV
    hidden_blocks = hidden_in.reshape(blocks, TOK_DEV, D)
    cot_blocks = cotangent.reshape(blocks, TOK_DEV, D)
    route_blocks = routes.reshape(blocks, TOK_DEV, TOP)
    gate_blocks = gate_values.reshape(blocks, TOK_DEV, TOP)

    def dispatch_block(inputs):
        hidden_rows, cot_rows, route_rows, gate_rows = inputs
        picker, weigher = slot_tables(route_rows, gate_rows)
        picker_half = picker.astype(jnp.bfloat16)
        slot_gate = lax.optimization_barrier(jnp.sum(weigher, axis=1))
        slot_in = jnp.dot(picker_half, hidden_rows, preferred_element_type=jnp.float32).astype(jnp.bfloat16)
        slot_cot = (jnp.dot(picker_half, cot_rows, preferred_element_type=jnp.float32) * slot_gate[:, None]).astype(jnp.bfloat16)
        return (slot_in, slot_cot, picker, weigher)
    slot_in, slot_cot, pickers, weighers = lax.map(dispatch_block, (hidden_blocks, cot_blocks, route_blocks, gate_blocks))
    in_by_expert = slot_in.reshape(blocks, EXPERTS, CAP, D).transpose(1, 0, 2, 3).reshape(EXPERTS, blocks * CAP, D)
    cot_by_expert = slot_cot.reshape(blocks, EXPERTS, CAP, D).transpose(1, 0, 2, 3).reshape(EXPERTS, blocks * CAP, D)

    def expert(inputs):
        in_rows, cot_rows, up_part, down_part = inputs
        pre = jnp.dot(in_rows, up_part, preferred_element_type=jnp.float32)
        activated = jax.nn.silu(pre).astype(jnp.bfloat16)
        slot_out = jnp.dot(activated, down_part, preferred_element_type=jnp.float32).astype(jnp.bfloat16)
        down_grad = jnp.dot(activated.T, cot_rows, preferred_element_type=jnp.float32).astype(jnp.bfloat16)
        act_grad = jnp.dot(cot_rows, down_part.T, preferred_element_type=jnp.float32)
        pre_grad = (act_grad * silu_grad(pre)).astype(jnp.bfloat16)
        up_grad = jnp.dot(in_rows.T, pre_grad, preferred_element_type=jnp.float32).astype(jnp.bfloat16)
        slot_in_grad = jnp.dot(pre_grad, up_part.T, preferred_element_type=jnp.float32).astype(jnp.bfloat16)
        return (slot_out, slot_in_grad, up_grad, down_grad)
    slot_out, slot_in_grad, up_grad, down_grad = lax.map(expert, (in_by_expert, cot_by_expert, up_weight, down_weight))
    out_blocks = slot_out.reshape(EXPERTS, blocks, CAP, D).transpose(1, 0, 2, 3).reshape(blocks, EXPERTS * CAP, D)
    grad_blocks = slot_in_grad.reshape(EXPERTS, blocks, CAP, D).transpose(1, 0, 2, 3).reshape(blocks, EXPERTS * CAP, D)

    def combine_block(inputs):
        hidden_rows, cot_rows, picker, weigher, out_rows, grad_rows = inputs
        gathered_out = jnp.dot(weigher.T, out_rows.astype(jnp.float32), precision=lax.Precision.HIGHEST)
        gathered_grad = jnp.dot(picker.T, grad_rows.astype(jnp.float32), precision=lax.Precision.HIGHEST)
        layer_rows = (hidden_rows.astype(jnp.float32) + gathered_out).astype(jnp.bfloat16)
        grad_back = (cot_rows.astype(jnp.float32) + gathered_grad).astype(jnp.bfloat16)
        return (layer_rows, grad_back)
    layer_out, input_grad = lax.map(combine_block, (hidden_blocks, cot_blocks, pickers, weighers, out_blocks, grad_blocks))
    return (layer_out.reshape(SEQS, LEN, D), input_grad.reshape(SEQS, LEN, D), up_grad, down_grad)
```

```python
import math

import jax
import jax.numpy as jnp
from jax import lax
from jax.sharding import Mesh
from jax.sharding import PartitionSpec as P

LAT = 512
HEADS = 2
CAP = 4
BLOCK = 128
EXPERTS = 16
CTX = ("zh", "y", "core")
EXP = ("zl", "x")
F32 = jnp.float32
BF16 = jnp.bfloat16


def swap(part, axis, mask):
    peers = lax.axis_size(axis)
    return lax.ppermute(part, axis, [(i, i ^ mask) for i in range(peers)])


def ordered(bit, mine, theirs, dim=0):
    low = jnp.where(bit == 0, mine, theirs)
    high = jnp.where(bit == 0, theirs, mine)
    return jnp.concatenate([low, high], axis=dim)


def add_rounded(a, b):
    return (a.astype(F32) + b.astype(F32)).astype(BF16)


def half_of(part, bit):
    rows = part.shape[0] // 2
    return lax.dynamic_slice_in_dim(part, bit * rows, rows, 0)


def sum_chips(part, bits):
    wide = part.shape[1] // 2
    orders = (((1, bits[0]), (3, bits[1])), ((3, bits[1]), (1, bits[0])))
    reduced = []
    for half, order in enumerate(orders):
        held = part[:, half * wide : (half + 1) * wide]
        for mask, bit in order:
            held = add_rounded(half_of(held, bit), swap(half_of(held, 1 - bit), "y", mask))
        reduced.append(held)
    reduced = [add_rounded(h, swap(h, "zh", 1)) for h in reduced]
    full = []
    for held, order in zip(reduced, orders):
        for mask, bit in reversed(order):
            held = ordered(bit, held, swap(held, "y", mask))
        full.append(held)
    return jnp.concatenate(full, axis=1)


def gather_relative(part, axis):
    wide = part.shape[-1] // 2
    halves = []
    for half, masks in enumerate(((1, 3), (3, 1))):
        held = part[..., half * wide : (half + 1) * wide][None]
        for mask in masks:
            held = jnp.concatenate([held, swap(held, axis, mask)], axis=0)
        if half == 1:
            held = jnp.stack([held[0], held[2], held[1], held[3]], axis=0)
        halves.append(held)
    return jnp.concatenate(halves, axis=-1)


def gather_ordered(part, axis, bits):
    wide = part.shape[-1] // 2
    first = part[..., :wide][None]
    first = ordered(bits[0], first, swap(first, axis, 1))
    first = ordered(bits[1], first, swap(first, axis, 3))
    second = part[..., wide:][None]
    second = ordered(bits[1], second, swap(second, axis, 3))
    theirs = swap(second, axis, 1)
    kind = bits[0] ^ bits[1]
    outer = jnp.where(kind == 0, second, theirs)
    inner = jnp.where(kind == 0, theirs, second)
    second = jnp.concatenate([outer[:1], inner, outer[1:]], axis=0)
    return jnp.concatenate([first, second], axis=-1)


def silu_grad(values_in):
    sigmoid_of = jax.nn.sigmoid(values_in)
    return sigmoid_of * (1.0 + values_in * (1.0 - sigmoid_of))


def slot_tables(route_rows, gate_rows):
    tokens = route_rows.shape[0]
    experts = jnp.arange(EXPERTS, dtype=jnp.int32)
    same = route_rows.T[None, :, :] == experts[:, None, None]
    hits = jnp.sum(same.astype(F32), axis=1)
    gates = jnp.sum(jnp.where(same, gate_rows.T[None, :, :], 0.0), axis=1)
    token_iota = jnp.arange(tokens, dtype=jnp.int32)
    earlier = (token_iota[:, None] < token_iota[None, :]).astype(BF16)
    rank = jnp.dot(hits.astype(BF16), earlier, preferred_element_type=F32)
    places = jnp.arange(CAP, dtype=jnp.int32).astype(F32)
    picked = (rank[:, None, :] == places[None, :, None]) & (hits[:, None, :] > 0.5)
    picker = picked.astype(F32).reshape(EXPERTS * CAP, tokens)
    weigher = jnp.where(picked, gates[:, None, :], 0.0).reshape(EXPERTS * CAP, tokens)
    return picker, weigher


def dispatched(slots, col_blocks):
    wide = slots.shape[1] // col_blocks
    pieces = slots.reshape(EXPERTS, CAP, col_blocks, wide).transpose(2, 0, 1, 3)
    pieces = pieces.reshape(col_blocks * EXPERTS, CAP, wide)
    pieces = lax.all_to_all(pieces, ("zh", "y") + EXP, split_axis=0, concat_axis=0, tiled=True)
    return pieces.reshape(col_blocks * EXPERTS * CAP, wide)


def returned(rows, col_blocks):
    wide = rows.shape[1]
    pieces = rows.reshape(col_blocks * EXPERTS, CAP, wide)
    pieces = lax.all_to_all(pieces, ("zh", "y") + EXP, split_axis=0, concat_axis=0, tiled=True)
    pieces = pieces.reshape(col_blocks, EXPERTS, CAP, wide).transpose(1, 2, 0, 3)
    return pieces.reshape(EXPERTS * CAP, col_blocks * wide)


def shards(
    residual,
    queries,
    latent,
    out_proj,
    up_weight,
    down_weight,
    cotangent,
    routes,
    gate_values,
    documents,
):
    zh = lax.axis_index("zh")
    y = lax.axis_index("y")
    core = lax.axis_index("core")
    x = lax.axis_index("x")
    y_bits = (y & 1, y >> 1)
    x_bits = (x & 1, x >> 1)
    tokens = residual.shape[1]
    model_width = residual.shape[2]
    col_blocks = 8
    wide = model_width // col_blocks
    inv_root = 1.0 / math.sqrt(LAT)

    own = latent[0]
    before = lax.ppermute(own, "zh", [(0, 1)])
    both = gather_relative(jnp.stack([own, before]), "y")
    y_xors = jnp.array([0, 1, 3, 2], jnp.int32)
    blocks_y = y ^ y_xors
    place = 2 * y + core
    held_place = 2 * blocks_y + core
    mine = jnp.where((held_place <= place)[:, None, None], both[:, 0], both[:, 1])
    for_partner = jnp.where(
        (held_place <= 2 * y + (1 - core))[:, None, None], both[:, 0], both[:, 1]
    )
    keys = jnp.concatenate([mine, swap(for_partner, "core", 1)], axis=0)
    keys = keys.reshape(8 * tokens, LAT)
    places = jnp.concatenate([held_place, 2 * blocks_y + (1 - core)])
    blocks = jnp.where(places <= place, zh * 8 + places, (zh - 1) * 8 + places)
    doc_row = documents[0]
    block_iota = jnp.arange(doc_row.shape[0], dtype=jnp.int32)
    block_docs = jnp.sum(
        jnp.where(blocks[:, None] == block_iota[None, :], doc_row[None, :], 0), axis=1
    )
    my_block = zh * 8 + place
    my_doc = jnp.sum(jnp.where(block_iota == my_block, doc_row, 0))
    block_open = (block_docs == my_doc) & (blocks >= 0) & (blocks <= my_block)
    token_iota = jnp.arange(tokens, dtype=jnp.int32)
    key_limit = jnp.where(
        block_open[:, None],
        jnp.where((blocks == my_block)[:, None], token_iota[None, :], -1),
        tokens,
    ).reshape(1, 8 * tokens)
    query_rows = jnp.concatenate([queries[0][:, :LAT], queries[0][:, LAT:]], axis=0)
    allowed = key_limit <= jnp.concatenate([token_iota, token_iota])[:, None]
    scores = (
        lax.dot_general(query_rows, keys, (((1,), (1,)), ((), ())), preferred_element_type=F32)
        * inv_root
    )
    scores = jnp.where(allowed, scores, -1e30)
    largest = jnp.max(scores, axis=1, keepdims=True)
    exponent = jnp.where(allowed, jnp.exp(scores - largest), 0.0)
    total = jnp.sum(exponent, axis=1, keepdims=True)
    mixed = jnp.dot(exponent.astype(BF16), keys, preferred_element_type=F32) / total
    mixed = mixed.astype(BF16)
    heads_out = jnp.concatenate([mixed[:tokens], mixed[tokens:]], axis=1)

    my_cols = 2 * x + core
    proj_rows = out_proj
    mine = lax.dynamic_slice_in_dim(proj_rows, my_cols * wide, wide, 1)
    theirs = lax.dynamic_slice_in_dim(proj_rows, (my_cols ^ 1) * wide, wide, 1)
    block_rows = ordered(core, mine, swap(theirs, "core", 1))
    block_rows = gather_ordered(block_rows, "y", y_bits).reshape(-1, wide)
    proj_block = ordered(zh, block_rows, swap(block_rows, "zh", 1))
    group_rows = ordered(core, heads_out, swap(heads_out, "core", 1))
    group_rows = gather_ordered(group_rows, "x", x_bits).reshape(8 * tokens, HEADS * LAT)
    projected = jnp.dot(group_rows, proj_block, preferred_element_type=F32).astype(BF16)
    projected = projected.reshape(8, tokens, wide)
    projected = lax.all_to_all(projected, ("x", "core"), split_axis=0, concat_axis=0, tiled=True)
    projected = projected.transpose(1, 0, 2).reshape(tokens, model_width)
    hidden_in = (residual[0].astype(F32) + projected.astype(F32)).astype(BF16)

    picker, weigher = slot_tables(routes[0], gate_values[0])
    picker_half = picker.astype(BF16)
    slot_gate = jnp.sum(weigher, axis=1)
    slot_cot = (
        jnp.dot(picker_half, cotangent[0], preferred_element_type=F32) * slot_gate[:, None]
    ).astype(BF16)
    cot_rows = dispatched(slot_cot, col_blocks)
    slot_in = jnp.dot(picker_half, hidden_in, preferred_element_type=F32).astype(BF16)
    in_rows = dispatched(slot_in, col_blocks)

    up_part = ordered(core, up_weight[0], swap(up_weight[0], "core", 1))
    down_part = ordered(core, down_weight[0], swap(down_weight[0], "core", 1), 1)
    contract_rows = (((0,), (0,)), ((), ()))
    contract_cols = (((1,), (1,)), ((), ()))
    grad_part = lax.dot_general(cot_rows, down_part, contract_cols, preferred_element_type=F32)
    sum_bits = (y_bits[0] ^ y_bits[1], y_bits[1])
    grad_full = sum_chips(grad_part.astype(BF16), sum_bits).astype(F32)
    pre_part = jnp.dot(in_rows, up_part, preferred_element_type=F32)
    pre_full = sum_chips(pre_part.astype(BF16), sum_bits).astype(F32)
    activated = jax.nn.silu(pre_full).astype(BF16)
    pre_grad = (grad_full * silu_grad(pre_full)).astype(BF16)
    slot_out = jnp.dot(activated, down_part, preferred_element_type=F32).astype(BF16)
    back_out = returned(slot_out, col_blocks)
    slot_in_grad = lax.dot_general(
        pre_grad, up_part, contract_cols, preferred_element_type=F32
    ).astype(BF16)
    back_grad = returned(slot_in_grad, col_blocks)

    down_both = lax.dot_general(activated, cot_rows, contract_rows, preferred_element_type=F32)
    part_width = wide // 2
    low, high = down_both[:, :part_width], down_both[:, part_width:]
    down_mine = jnp.where(core == 0, low, high)
    down_theirs = jnp.where(core == 0, high, low).astype(BF16)
    down_grad = (down_mine + swap(down_theirs, "core", 1).astype(F32)).astype(BF16)
    up_both = lax.dot_general(in_rows, pre_grad, contract_rows, preferred_element_type=F32)
    up_mine = half_of(up_both, core)
    up_theirs = half_of(up_both, 1 - core).astype(BF16)
    up_grad = (up_mine + swap(up_theirs, "core", 1).astype(F32)).astype(BF16)

    gate_high = weigher.astype(BF16)
    gate_low = (weigher - gate_high.astype(F32)).astype(BF16)
    gathered_out = lax.dot_general(
        jnp.concatenate([gate_high, gate_low], axis=0),
        jnp.concatenate([back_out, back_out], axis=0),
        contract_rows,
        preferred_element_type=F32,
    )
    gathered_grad = lax.dot_general(
        picker_half, back_grad, contract_rows, preferred_element_type=F32
    )
    layer_out = (hidden_in.astype(F32) + gathered_out).astype(BF16)
    input_grad = (cotangent[0].astype(F32) + gathered_grad).astype(BF16)
    return (layer_out[None], input_grad[None], up_grad[None], down_grad[None])


def solution(mesh):
    grid = Mesh(mesh.devices.reshape(2, 4, 2, 4, 4), CTX + EXP)
    placed = (
        P(EXP, CTX, None),
        P(EXP, CTX, None),
        P(EXP, CTX, None),
        P(CTX, None),
        P(EXP, CTX, None),
        P(EXP, None, CTX),
        P(EXP, CTX, None),
        P(EXP, CTX, None),
        P(EXP, CTX, None),
        P(EXP, None),
    )
    return jax.shard_map(
        shards,
        mesh=grid,
        in_specs=placed,
        out_specs=(
            P(EXP, CTX, None),
            P(EXP, CTX, None),
            P(EXP, CTX, None),
            P(EXP, None, CTX),
        ),
        check_vma=False,
    )
```

```python
import math

import jax
import jax.numpy as jnp
from jax import lax
from jax.sharding import Mesh
from jax.sharding import PartitionSpec as P


LAT = 512
HEADS = 2
CAP = 4
EXPERTS = 16
CTX = ("zh", "y", "core")
EXP = ("zl", "x")
F32 = jnp.float32
BF16 = jnp.bfloat16


def swap(part, axis, mask):
    peers = lax.axis_size(axis)
    return lax.ppermute(part, axis, [(i, i ^ mask) for i in range(peers)])


def ordered(bit, mine, theirs, dim=0):
    low = jnp.where(bit == 0, mine, theirs)
    high = jnp.where(bit == 0, theirs, mine)
    return jnp.concatenate([low, high], axis=dim)


def add_rounded(a, b):
    return (a.astype(F32) + b.astype(F32)).astype(BF16)


def half_of(part, bit):
    rows = part.shape[0] // 2
    return lax.dynamic_slice_in_dim(part, bit * rows, rows, 0)


def sum_chips(part, bits):
    wide = part.shape[1] // 2
    orders = (((1, bits[0]), (3, bits[1])), ((3, bits[1]), (1, bits[0])))
    reduced = []
    for half, order in enumerate(orders):
        held = part[:, half * wide : (half + 1) * wide]
        for mask, bit in order:
            held = add_rounded(half_of(held, bit), swap(half_of(held, 1 - bit), "y", mask))
        reduced.append(held)
    reduced = [add_rounded(h, swap(h, "zh", 1)) for h in reduced]
    full = []
    for held, order in zip(reduced, orders):
        for mask, bit in reversed(order):
            held = ordered(bit, held, swap(held, "y", mask))
        full.append(held)
    return jnp.concatenate(full, axis=1)


def gather_relative(part, axis):
    wide = part.shape[-1] // 2
    halves = []
    for half, masks in enumerate(((1, 3), (3, 1))):
        held = part[..., half * wide : (half + 1) * wide][None]
        for mask in masks:
            held = jnp.concatenate([held, swap(held, axis, mask)], axis=0)
        if half == 1:
            held = jnp.stack([held[0], held[2], held[1], held[3]], axis=0)
        halves.append(held)
    return jnp.concatenate(halves, axis=-1)


def gather_ordered(part, axis, bits):
    wide = part.shape[-1] // 2
    first = part[..., :wide][None]
    first = ordered(bits[0], first, swap(first, axis, 1))
    first = ordered(bits[1], first, swap(first, axis, 3))
    second = part[..., wide:][None]
    second = ordered(bits[1], second, swap(second, axis, 3))
    theirs = swap(second, axis, 1)
    kind = bits[0] ^ bits[1]
    outer = jnp.where(kind == 0, second, theirs)
    inner = jnp.where(kind == 0, theirs, second)
    second = jnp.concatenate([outer[:1], inner, outer[1:]], axis=0)
    return jnp.concatenate([first, second], axis=-1)


def mirror_z(part):
    return lax.ppermute(part, ("zh", "zl"), [(i, 7 - i) for i in range(8)])


def by_source(pieces, bits):
    pieces = [jnp.where(bits[0] == 0, pieces[m], pieces[m ^ 1]) for m in range(4)]
    return jnp.stack([jnp.where(bits[1] == 0, pieces[m], pieces[m ^ 2]) for m in range(4)])


def exchange(pieces, axis, index, bits):
    got = [lax.dynamic_index_in_dim(pieces, index, 0, keepdims=False)]
    for mask in (1, 2, 3):
        got.append(swap(lax.dynamic_index_in_dim(pieces, index ^ mask, 0, False), axis, mask))
    return by_source(got, bits)


def col_piece(part, index, wide):
    return lax.dynamic_slice_in_dim(part, index * wide, wide, part.ndim - 1)


def silu_grad(values_in):
    sigmoid_of = jax.nn.sigmoid(values_in)
    return sigmoid_of * (1.0 + values_in * (1.0 - sigmoid_of))


def slot_tables(route_rows, gate_rows):
    tokens = route_rows.shape[0]
    experts = jnp.arange(EXPERTS, dtype=jnp.int32)
    same = route_rows.T[None, :, :] == experts[:, None, None]
    hits = jnp.sum(same.astype(F32), axis=1)
    gates = jnp.sum(jnp.where(same, gate_rows.T[None, :, :], 0.0), axis=1)
    token_iota = jnp.arange(tokens, dtype=jnp.int32)
    earlier = (token_iota[:, None] < token_iota[None, :]).astype(BF16)
    rank = jnp.dot(hits.astype(BF16), earlier, preferred_element_type=F32)
    places = jnp.arange(CAP, dtype=jnp.int32).astype(F32)
    picked = (rank[:, None, :] == places[None, :, None]) & (hits[:, None, :] > 0.5)
    picker = picked.astype(F32).reshape(EXPERTS * CAP, tokens)
    weigher = jnp.where(picked, gates[:, None, :], 0.0).reshape(EXPERTS * CAP, tokens)
    return picker, weigher


def dispatched(slots, col_blocks):
    wide = slots.shape[1] // col_blocks
    pieces = slots.reshape(EXPERTS, CAP, col_blocks, wide).transpose(2, 0, 1, 3)
    pieces = pieces.reshape(col_blocks * EXPERTS, CAP, wide)
    pieces = lax.all_to_all(pieces, ("zh", "y") + EXP, split_axis=0, concat_axis=0, tiled=True)
    return pieces.reshape(col_blocks * EXPERTS * CAP, wide)


def returned(rows, col_blocks):
    wide = rows.shape[1]
    pieces = rows.reshape(col_blocks * EXPERTS, CAP, wide)
    pieces = lax.all_to_all(pieces, ("zh", "y") + EXP, split_axis=0, concat_axis=0, tiled=True)
    pieces = pieces.reshape(col_blocks, EXPERTS, CAP, wide).transpose(1, 2, 0, 3)
    return pieces.reshape(EXPERTS * CAP, col_blocks * wide)


def shards(
    residual,
    queries,
    latent,
    out_proj,
    up_weight,
    down_weight,
    cotangent,
    routes,
    gate_values,
    documents,
):
    zh = lax.axis_index("zh")
    y = lax.axis_index("y")
    core = lax.axis_index("core")
    x = lax.axis_index("x")
    y_bits = (y & 1, y >> 1)
    x_bits = (x & 1, x >> 1)
    tokens = residual.shape[1]
    model_width = residual.shape[2]
    col_blocks = 8
    wide = model_width // col_blocks
    inv_root = 1.0 / math.sqrt(LAT)

    own = latent[0]
    before = lax.ppermute(own, "zh", [(0, 1)])
    both = gather_relative(jnp.stack([own, before]), "y")
    y_xors = jnp.array([0, 1, 3, 2], jnp.int32)
    blocks_y = y ^ y_xors
    place = 2 * y + core
    held_place = 2 * blocks_y + core
    mine = jnp.where((held_place <= place)[:, None, None], both[:, 0], both[:, 1])
    for_partner = jnp.where(
        (held_place <= 2 * y + (1 - core))[:, None, None], both[:, 0], both[:, 1]
    )
    theirs = swap(for_partner, "core", 1)
    keys = jnp.concatenate([mine, theirs], axis=0)
    keys = keys.reshape(8 * tokens, LAT)
    places = jnp.concatenate([held_place, 2 * blocks_y + (1 - core)])
    blocks = jnp.where(places <= place, zh * 8 + places, (zh - 1) * 8 + places)
    doc_row = documents[0]
    block_iota = jnp.arange(doc_row.shape[0], dtype=jnp.int32)
    block_docs = jnp.sum(
        jnp.where(blocks[:, None] == block_iota[None, :], doc_row[None, :], 0), axis=1
    )
    my_block = zh * 8 + place
    my_doc = jnp.sum(jnp.where(block_iota == my_block, doc_row, 0))
    block_open = (block_docs == my_doc) & (blocks >= 0) & (blocks <= my_block)
    token_iota = jnp.arange(tokens, dtype=jnp.int32)
    key_limit = jnp.where(
        block_open[:, None],
        jnp.where((blocks == my_block)[:, None], token_iota[None, :], -1),
        tokens,
    ).reshape(1, 8 * tokens)
    query_rows = jnp.concatenate([queries[0][:, :LAT], queries[0][:, LAT:]], axis=0)
    allowed = key_limit <= jnp.concatenate([token_iota, token_iota])[:, None]
    scores = (
        lax.dot_general(query_rows, keys, (((1,), (1,)), ((), ())), preferred_element_type=F32)
        * inv_root
    )
    scores = jnp.where(allowed, scores, -1e30)
    largest = jnp.max(scores, axis=1, keepdims=True)
    exponent = jnp.where(allowed, jnp.exp(scores - largest), 0.0)
    total = jnp.sum(exponent, axis=1, keepdims=True)
    mixed = jnp.dot(exponent.astype(BF16), keys, preferred_element_type=F32) / total
    mixed = mixed.astype(BF16)
    heads_out = jnp.concatenate([mixed[:tokens], mixed[tokens:]], axis=1)

    picker, weigher = slot_tables(routes[0], gate_values[0])
    picker_half = picker.astype(BF16)
    slot_gate = jnp.sum(weigher, axis=1)
    slot_cot = (
        jnp.dot(picker_half, cotangent[0], preferred_element_type=F32) * slot_gate[:, None]
    ).astype(BF16)
    slot_res = jnp.dot(picker_half, residual[0], preferred_element_type=F32).astype(BF16)
    cot_rows = dispatched(slot_cot, col_blocks)
    res_rows = dispatched(slot_res, col_blocks)

    half_width = model_width // 2
    cols_src, _ = lax.optimization_barrier((out_proj, before))
    cols_mine = lax.dynamic_slice_in_dim(cols_src, zh * half_width, half_width, 1)
    cols_other = lax.dynamic_slice_in_dim(cols_src, (1 - zh) * half_width, half_width, 1)
    half_rows = ordered(zh, cols_mine[None], mirror_z(cols_other)[None])
    pieces = [col_piece(half_rows, y, wide)]
    for mask in (1, 2, 3):
        pieces.append(swap(col_piece(half_rows, y ^ mask, wide), "y", mask))
    by_y = by_source(pieces, y_bits)
    by_core = ordered(core, by_y[None], swap(by_y, "core", 1)[None])
    chip_cols = by_core.transpose(2, 1, 0, 3, 4).reshape(HEADS * LAT, wide)

    slot_heads = jnp.dot(picker_half, heads_out, preferred_element_type=F32).astype(BF16)
    zl = lax.axis_index("zl")
    by_x = exchange(slot_heads.reshape(4, 4, CAP, -1).transpose(1, 0, 2, 3), "x", x, x_bits)
    by_z = exchange(by_x.transpose(1, 0, 2, 3), "zl", zl, (zl & 1, zl >> 1))
    heads_rows = by_z.reshape(EXPERTS * CAP, HEADS * LAT)
    heads_rows = gather_ordered(heads_rows, "y", y_bits).reshape(-1, HEADS * LAT)
    heads_rows = ordered(zh, heads_rows, swap(heads_rows, "zh", 1))
    in_rows = (
        res_rows.astype(F32) + jnp.dot(heads_rows, chip_cols, preferred_element_type=F32)
    ).astype(BF16)

    my_cols = 2 * x + core
    proj_rows, _ = lax.optimization_barrier((out_proj, slot_heads))
    mine = lax.dynamic_slice_in_dim(proj_rows, my_cols * wide, wide, 1)
    theirs = lax.dynamic_slice_in_dim(proj_rows, (my_cols ^ 1) * wide, wide, 1)
    block_rows = ordered(core, mine, swap(theirs, "core", 1))
    block_rows = gather_ordered(block_rows, "y", y_bits).reshape(-1, wide)
    proj_block = ordered(zh, block_rows, mirror_z(block_rows))
    group_rows = ordered(core, heads_out, swap(heads_out, "core", 1))
    group_rows = gather_ordered(group_rows, "x", x_bits).reshape(8 * tokens, HEADS * LAT)
    projected = jnp.dot(group_rows, proj_block, preferred_element_type=F32).astype(BF16)
    projected = projected.reshape(8, tokens, wide)
    projected = lax.all_to_all(projected, ("x", "core"), split_axis=0, concat_axis=0, tiled=True)
    projected = projected.transpose(1, 0, 2).reshape(tokens, model_width)
    hidden_in = (residual[0].astype(F32) + projected.astype(F32)).astype(BF16)

    up_own, down_own, _ = lax.optimization_barrier((up_weight[0], down_weight[0], keys))
    up_part = ordered(core, up_own, swap(up_own, "core", 1))
    down_part = ordered(core, down_own, swap(down_own, "core", 1), 1)
    contract_rows = (((0,), (0,)), ((), ()))
    contract_cols = (((1,), (1,)), ((), ()))
    grad_part = lax.dot_general(cot_rows, down_part, contract_cols, preferred_element_type=F32)
    sum_bits = (y_bits[0] ^ y_bits[1], y_bits[1])
    grad_full = sum_chips(grad_part.astype(BF16), sum_bits).astype(F32)
    pre_part = jnp.dot(in_rows, up_part, preferred_element_type=F32)
    pre_full = sum_chips(pre_part.astype(BF16), sum_bits).astype(F32)
    activated = jax.nn.silu(pre_full).astype(BF16)
    pre_grad = (grad_full * silu_grad(pre_full)).astype(BF16)
    slot_out = jnp.dot(activated, down_part, preferred_element_type=F32).astype(BF16)
    back_out = returned(slot_out, col_blocks)
    slot_in_grad = lax.dot_general(
        pre_grad, up_part, contract_cols, preferred_element_type=F32
    ).astype(BF16)
    back_grad = returned(slot_in_grad, col_blocks)

    down_both = lax.dot_general(activated, cot_rows, contract_rows, preferred_element_type=F32)
    part_width = wide // 2
    low, high = down_both[:, :part_width], down_both[:, part_width:]
    down_mine = jnp.where(core == 0, low, high)
    down_theirs = jnp.where(core == 0, high, low).astype(BF16)
    down_grad = (down_mine + swap(down_theirs, "core", 1).astype(F32)).astype(BF16)
    up_both = lax.dot_general(in_rows, pre_grad, contract_rows, preferred_element_type=F32)
    up_mine = half_of(up_both, core)
    up_theirs = half_of(up_both, 1 - core).astype(BF16)
    up_grad = (up_mine + swap(up_theirs, "core", 1).astype(F32)).astype(BF16)

    gate_high = weigher.astype(BF16)
    gate_low = (weigher - gate_high.astype(F32)).astype(BF16)
    gathered_out = lax.dot_general(
        jnp.concatenate([gate_high, gate_low], axis=0),
        jnp.concatenate([back_out, back_out], axis=0),
        contract_rows,
        preferred_element_type=F32,
    )
    gathered_grad = lax.dot_general(
        picker_half, back_grad, contract_rows, preferred_element_type=F32
    )
    layer_out = (hidden_in.astype(F32) + gathered_out).astype(BF16)
    input_grad = (cotangent[0].astype(F32) + gathered_grad).astype(BF16)
    return (layer_out[None], input_grad[None], up_grad[None], down_grad[None])


def solution(mesh):
    grid = Mesh(mesh.devices.reshape(2, 4, 2, 4, 4), CTX + EXP)
    placed = (
        P(EXP, CTX, None),
        P(EXP, CTX, None),
        P(EXP, CTX, None),
        P(CTX, None),
        P(EXP, CTX, None),
        P(EXP, None, CTX),
        P(EXP, CTX, None),
        P(EXP, CTX, None),
        P(EXP, CTX, None),
        P(EXP, None),
    )

    return jax.shard_map(
        shards,
        mesh=grid,
        in_specs=placed,
        out_specs=(
            P(EXP, CTX, None),
            P(EXP, CTX, None),
            P(EXP, CTX, None),
            P(EXP, None, CTX),
        ),
        check_vma=False,
    )
```

```python
import math

import jax
import jax.numpy as jnp
from jax import lax
from jax.sharding import Mesh
from jax.sharding import PartitionSpec as P


LAT = 512
HEADS = 2
CAP = 4
EXPERTS = 16
CTX = ("zh", "y", "core")
EXP = ("zl", "x")
F32 = jnp.float32
BF16 = jnp.bfloat16


def swap(part, axis, mask):
    peers = lax.axis_size(axis)
    return lax.ppermute(part, axis, [(i, i ^ mask) for i in range(peers)])


def ordered(bit, mine, theirs, dim=0):
    low = jnp.where(bit == 0, mine, theirs)
    high = jnp.where(bit == 0, theirs, mine)
    return jnp.concatenate([low, high], axis=dim)


def add_rounded(a, b):
    return (a.astype(F32) + b.astype(F32)).astype(BF16)


def half_of(part, bit):
    rows = part.shape[0] // 2
    return lax.dynamic_slice_in_dim(part, bit * rows, rows, 0)


def sum_chips(part, bits):
    wide = part.shape[1] // 2
    orders = (((1, bits[0]), (3, bits[1])), ((3, bits[1]), (1, bits[0])))
    reduced = []
    for half, order in enumerate(orders):
        held = part[:, half * wide : (half + 1) * wide]
        for mask, bit in order:
            held = add_rounded(half_of(held, bit), swap(half_of(held, 1 - bit), "y", mask))
        reduced.append(held)
    reduced = [add_rounded(h, swap(h, "zh", 1)) for h in reduced]
    full = []
    for held, order in zip(reduced, orders):
        for mask, bit in reversed(order):
            held = ordered(bit, held, swap(held, "y", mask))
        full.append(held)
    return jnp.concatenate(full, axis=1)


def gather_relative(part, axis):
    wide = part.shape[-1] // 2
    halves = []
    for half, masks in enumerate(((1, 3), (3, 1))):
        held = part[..., half * wide : (half + 1) * wide][None]
        for mask in masks:
            held = jnp.concatenate([held, swap(held, axis, mask)], axis=0)
        if half == 1:
            held = jnp.stack([held[0], held[2], held[1], held[3]], axis=0)
        halves.append(held)
    return jnp.concatenate(halves, axis=-1)


def gather_ordered(part, axis, bits):
    wide = part.shape[-1] // 2
    first = part[..., :wide][None]
    first = ordered(bits[0], first, swap(first, axis, 1))
    first = ordered(bits[1], first, swap(first, axis, 3))
    second = part[..., wide:][None]
    second = ordered(bits[1], second, swap(second, axis, 3))
    theirs = swap(second, axis, 1)
    kind = bits[0] ^ bits[1]
    outer = jnp.where(kind == 0, second, theirs)
    inner = jnp.where(kind == 0, theirs, second)
    second = jnp.concatenate([outer[:1], inner, outer[1:]], axis=0)
    return jnp.concatenate([first, second], axis=-1)


def mirror_z(part):
    return lax.ppermute(part, ("zh", "zl"), [(i, 7 - i) for i in range(8)])


def by_source(pieces, bits):
    for place, bit in enumerate(bits):
        pieces = [
            jnp.where(bit == 0, pieces[m], pieces[m ^ (1 << place)]) for m in range(len(pieces))
        ]
    return jnp.stack(pieces)


def exchange(pieces, axis, index, bits):
    got = [lax.dynamic_index_in_dim(pieces, index, 0, keepdims=False)]
    for mask in (1, 2, 3):
        got.append(swap(lax.dynamic_index_in_dim(pieces, index ^ mask, 0, False), axis, mask))
    return by_source(got, bits)


def col_piece(part, index, wide):
    return lax.dynamic_slice_in_dim(part, index * wide, wide, part.ndim - 1)


def silu_grad(values_in):
    sigmoid_of = jax.nn.sigmoid(values_in)
    return sigmoid_of * (1.0 + values_in * (1.0 - sigmoid_of))


def slot_tables(route_rows, gate_rows):
    tokens = route_rows.shape[0]
    experts = jnp.arange(EXPERTS, dtype=jnp.int32)
    same = route_rows.T[None, :, :] == experts[:, None, None]
    hits = jnp.sum(same.astype(F32), axis=1)
    gates = jnp.sum(jnp.where(same, gate_rows.T[None, :, :], 0.0), axis=1)
    token_iota = jnp.arange(tokens, dtype=jnp.int32)
    earlier = (token_iota[:, None] < token_iota[None, :]).astype(BF16)
    rank = jnp.dot(hits.astype(BF16), earlier, preferred_element_type=F32)
    places = jnp.arange(CAP, dtype=jnp.int32).astype(F32)
    picked = (rank[:, None, :] == places[None, :, None]) & (hits[:, None, :] > 0.5)
    picker = picked.astype(F32).reshape(EXPERTS * CAP, tokens)
    weigher = jnp.where(picked, gates[:, None, :], 0.0).reshape(EXPERTS * CAP, tokens)
    return picker, weigher


def dispatched(slots, col_blocks):
    wide = slots.shape[1] // col_blocks
    pieces = slots.reshape(EXPERTS, CAP, col_blocks, wide).transpose(2, 0, 1, 3)
    pieces = pieces.reshape(col_blocks * EXPERTS, CAP, wide)
    pieces = lax.all_to_all(pieces, ("zh", "y") + EXP, split_axis=0, concat_axis=0, tiled=True)
    return pieces.reshape(col_blocks * EXPERTS * CAP, wide)


def returned(rows, col_blocks):
    wide = rows.shape[1]
    pieces = rows.reshape(col_blocks * EXPERTS, CAP, wide)
    pieces = lax.all_to_all(pieces, ("zh", "y") + EXP, split_axis=0, concat_axis=0, tiled=True)
    pieces = pieces.reshape(col_blocks, EXPERTS, CAP, wide).transpose(1, 2, 0, 3)
    return pieces.reshape(EXPERTS * CAP, col_blocks * wide)


def shards(
    residual,
    queries,
    latent,
    out_proj,
    up_weight,
    down_weight,
    cotangent,
    routes,
    gate_values,
    documents,
):
    zh = lax.axis_index("zh")
    y = lax.axis_index("y")
    core = lax.axis_index("core")
    x = lax.axis_index("x")
    y_bits = (y & 1, y >> 1)
    x_bits = (x & 1, x >> 1)
    tokens = residual.shape[1]
    model_width = residual.shape[2]
    col_blocks = 8
    wide = model_width // col_blocks
    inv_root = 1.0 / math.sqrt(LAT)

    own = latent[0]
    before = lax.ppermute(own, "zh", [(0, 1)])
    both = gather_relative(jnp.stack([own, before]), "y")
    y_xors = jnp.array([0, 1, 3, 2], jnp.int32)
    blocks_y = y ^ y_xors
    place = 2 * y + core
    held_place = 2 * blocks_y + core
    mine = jnp.where((held_place <= place)[:, None, None], both[:, 0], both[:, 1])
    for_partner = jnp.where(
        (held_place <= 2 * y + (1 - core))[:, None, None], both[:, 0], both[:, 1]
    )
    theirs = swap(for_partner, "core", 1)
    keys = jnp.concatenate([mine, theirs], axis=0)
    keys = keys.reshape(8 * tokens, LAT)
    places = jnp.concatenate([held_place, 2 * blocks_y + (1 - core)])
    blocks = jnp.where(places <= place, zh * 8 + places, (zh - 1) * 8 + places)
    doc_row = documents[0]
    block_iota = jnp.arange(doc_row.shape[0], dtype=jnp.int32)
    block_docs = jnp.sum(
        jnp.where(blocks[:, None] == block_iota[None, :], doc_row[None, :], 0), axis=1
    )
    my_block = zh * 8 + place
    my_doc = jnp.sum(jnp.where(block_iota == my_block, doc_row, 0))
    block_open = (block_docs == my_doc) & (blocks >= 0) & (blocks <= my_block)
    token_iota = jnp.arange(tokens, dtype=jnp.int32)
    key_limit = jnp.where(
        block_open[:, None],
        jnp.where((blocks == my_block)[:, None], token_iota[None, :], -1),
        tokens,
    ).reshape(1, 8 * tokens)
    query_rows = jnp.concatenate([queries[0][:, :LAT], queries[0][:, LAT:]], axis=0)
    allowed = key_limit <= jnp.concatenate([token_iota, token_iota])[:, None]
    scores = (
        lax.dot_general(query_rows, keys, (((1,), (1,)), ((), ())), preferred_element_type=F32)
        * inv_root
    )
    scores = jnp.where(allowed, scores, -1e30)
    largest = jnp.max(scores, axis=1, keepdims=True)
    exponent = jnp.where(allowed, jnp.exp(scores - largest), 0.0)
    total = jnp.sum(exponent, axis=1, keepdims=True)
    mixed = jnp.dot(exponent.astype(BF16), keys, preferred_element_type=F32) / total
    mixed = mixed.astype(BF16)
    heads_out = jnp.concatenate([mixed[:tokens], mixed[tokens:]], axis=1)

    picker, weigher = slot_tables(routes[0], gate_values[0])
    picker_half = picker.astype(BF16)
    slot_gate = jnp.sum(weigher, axis=1)
    slot_cot = (
        jnp.dot(picker_half, cotangent[0], preferred_element_type=F32) * slot_gate[:, None]
    ).astype(BF16)
    slot_res = jnp.dot(picker_half, residual[0], preferred_element_type=F32).astype(BF16)
    cot_rows = dispatched(slot_cot, col_blocks)
    res_rows = dispatched(slot_res, col_blocks)

    half_width = model_width // 2
    cols_src = out_proj
    cols_mine = lax.dynamic_slice_in_dim(cols_src, zh * half_width, half_width, 1)
    cols_other = lax.dynamic_slice_in_dim(cols_src, (1 - zh) * half_width, half_width, 1)
    half_rows = ordered(zh, cols_mine[None], mirror_z(cols_other)[None])
    slot_heads = jnp.dot(picker_half, heads_out, preferred_element_type=F32).astype(BF16)
    zl = lax.axis_index("zl")
    by_x = exchange(slot_heads.reshape(4, 4, CAP, -1).transpose(1, 0, 2, 3), "x", x, x_bits)
    by_z = exchange(by_x.transpose(1, 0, 2, 3), "zl", zl, (zl & 1, zl >> 1))
    heads_rows_own = by_z.reshape(EXPERTS * CAP, HEADS * LAT)
    heads_rows = gather_ordered(heads_rows_own, "y", y_bits).reshape(-1, HEADS * LAT)
    heads_rows = ordered(zh, heads_rows, swap(heads_rows, "zh", 1))
    pieces = [col_piece(half_rows, y, wide)]
    for mask in (1, 2, 3):
        pieces.append(swap(col_piece(half_rows, y ^ mask, wide), "y", mask))
    by_y = by_source(pieces, y_bits)
    by_core = ordered(core, by_y[None], swap(by_y, "core", 1)[None])
    chip_cols = by_core.transpose(2, 1, 0, 3, 4).reshape(HEADS * LAT, wide)
    in_rows = (
        res_rows.astype(F32) + jnp.dot(heads_rows, chip_cols, preferred_element_type=F32)
    ).astype(BF16)

    my_cols = 2 * x + core
    proj_rows, group_heads = out_proj, heads_out
    mine = lax.dynamic_slice_in_dim(proj_rows, my_cols * wide, wide, 1)
    theirs = lax.dynamic_slice_in_dim(proj_rows, (my_cols ^ 1) * wide, wide, 1)
    block_rows = ordered(core, mine, swap(theirs, "core", 1))
    block_rows = gather_ordered(block_rows, "y", y_bits).reshape(-1, wide)
    proj_block = ordered(zh, block_rows, mirror_z(block_rows))
    group_rows = ordered(core, group_heads, swap(group_heads, "core", 1))
    group_rows = gather_ordered(group_rows, "x", x_bits).reshape(8 * tokens, HEADS * LAT)
    projected = jnp.dot(group_rows, proj_block, preferred_element_type=F32).astype(BF16)
    projected = projected.reshape(8, tokens, wide)
    parts = [lax.dynamic_index_in_dim(projected, my_cols, 0, keepdims=False)]
    for mask in range(1, 8):
        part = lax.dynamic_index_in_dim(projected, my_cols ^ mask, 0, keepdims=False)
        flip = (mask & 1) * 4 + (mask >> 1)
        parts.append(lax.ppermute(part, ("core", "x"), [(i, i ^ flip) for i in range(8)]))
    projected = by_source(parts, (core,) + x_bits)
    projected = projected.transpose(1, 0, 2).reshape(tokens, model_width)
    hidden_in = (residual[0].astype(F32) + projected.astype(F32)).astype(BF16)

    up_own, down_own = up_weight[0], down_weight[0]
    up_part = ordered(core, up_own, swap(up_own, "core", 1))
    down_part = ordered(core, down_own, swap(down_own, "core", 1), 1)
    contract_rows = (((0,), (0,)), ((), ()))
    contract_cols = (((1,), (1,)), ((), ()))
    grad_part = lax.dot_general(cot_rows, down_part, contract_cols, preferred_element_type=F32)
    sum_bits = (y_bits[0] ^ y_bits[1], y_bits[1])
    grad_full = sum_chips(grad_part.astype(BF16), sum_bits).astype(F32)
    pre_part = jnp.dot(in_rows, up_part, preferred_element_type=F32)
    pre_full = sum_chips(pre_part.astype(BF16), sum_bits).astype(F32)
    activated = jax.nn.silu(pre_full).astype(BF16)
    pre_grad = (grad_full * silu_grad(pre_full)).astype(BF16)
    slot_out = jnp.dot(activated, down_part, preferred_element_type=F32).astype(BF16)
    back_out = returned(slot_out, col_blocks)
    slot_in_grad = lax.dot_general(
        pre_grad, up_part, contract_cols, preferred_element_type=F32
    ).astype(BF16)
    back_grad = returned(slot_in_grad, col_blocks)

    down_both = lax.dot_general(activated, cot_rows, contract_rows, preferred_element_type=F32)
    part_width = wide // 2
    low, high = down_both[:, :part_width], down_both[:, part_width:]
    down_mine = jnp.where(core == 0, low, high)
    down_theirs = jnp.where(core == 0, high, low).astype(BF16)
    down_grad = (down_mine + swap(down_theirs, "core", 1).astype(F32)).astype(BF16)
    up_both = lax.dot_general(in_rows, pre_grad, contract_rows, preferred_element_type=F32)
    up_mine = half_of(up_both, core)
    up_theirs = half_of(up_both, 1 - core).astype(BF16)
    up_grad = (up_mine + swap(up_theirs, "core", 1).astype(F32)).astype(BF16)

    gate_high = weigher.astype(BF16)
    gate_low = (weigher - gate_high.astype(F32)).astype(BF16)
    gathered_out = lax.dot_general(
        jnp.concatenate([gate_high, gate_low], axis=0),
        jnp.concatenate([back_out, back_out], axis=0),
        contract_rows,
        preferred_element_type=F32,
    )
    gathered_grad = lax.dot_general(
        picker_half, back_grad, contract_rows, preferred_element_type=F32
    )
    layer_out = (hidden_in.astype(F32) + gathered_out).astype(BF16)
    input_grad = (cotangent[0].astype(F32) + gathered_grad).astype(BF16)
    return (layer_out[None], input_grad[None], up_grad[None], down_grad[None])


def solution(mesh):
    grid = Mesh(mesh.devices.reshape(2, 4, 2, 4, 4), CTX + EXP)
    placed = (
        P(EXP, CTX, None),
        P(EXP, CTX, None),
        P(EXP, CTX, None),
        P(CTX, None),
        P(EXP, CTX, None),
        P(EXP, None, CTX),
        P(EXP, CTX, None),
        P(EXP, CTX, None),
        P(EXP, CTX, None),
        P(EXP, None),
    )

    return jax.shard_map(
        shards,
        mesh=grid,
        in_specs=placed,
        out_specs=(
            P(EXP, CTX, None),
            P(EXP, CTX, None),
            P(EXP, CTX, None),
            P(EXP, None, CTX),
        ),
        check_vma=False,
    )
```

```python
import math

import jax
import jax.numpy as jnp
from jax import lax
from jax.sharding import Mesh
from jax.sharding import PartitionSpec as P


LAT = 512
HEADS = 2
CAP = 4
EXPERTS = 16
CTX = ("zh", "y", "core")
EXP = ("zl", "x")
F32 = jnp.float32
BF16 = jnp.bfloat16


def swap(part, axis, mask):
    peers = lax.axis_size(axis)
    return lax.ppermute(part, axis, [(i, i ^ mask) for i in range(peers)])


def ordered(bit, mine, theirs, dim=0):
    low = jnp.where(bit == 0, mine, theirs)
    high = jnp.where(bit == 0, theirs, mine)
    return jnp.concatenate([low, high], axis=dim)


def add_rounded(a, b):
    return (a.astype(F32) + b.astype(F32)).astype(BF16)


def half_of(part, bit):
    rows = part.shape[0] // 2
    return lax.dynamic_slice_in_dim(part, bit * rows, rows, 0)


def sum_chips(part, bits):
    wide = part.shape[1] // 2
    orders = (((1, bits[0]), (3, bits[1])), ((3, bits[1]), (1, bits[0])))
    reduced = []
    for half, order in enumerate(orders):
        held = part[:, half * wide : (half + 1) * wide]
        for mask, bit in order:
            held = add_rounded(half_of(held, bit), swap(half_of(held, 1 - bit), "y", mask))
        reduced.append(held)
    reduced = [add_rounded(h, swap(h, "zh", 1)) for h in reduced]
    full = []
    for held, order in zip(reduced, orders):
        for mask, bit in reversed(order):
            held = ordered(bit, held, swap(held, "y", mask))
        full.append(held)
    return jnp.concatenate(full, axis=1)


def gather_relative(part, axis):
    wide = part.shape[-1] // 2
    halves = []
    for half, masks in enumerate(((1, 3), (3, 1))):
        held = part[..., half * wide : (half + 1) * wide][None]
        for mask in masks:
            held = jnp.concatenate([held, swap(held, axis, mask)], axis=0)
        if half == 1:
            held = jnp.stack([held[0], held[2], held[1], held[3]], axis=0)
        halves.append(held)
    return jnp.concatenate(halves, axis=-1)


def gather_ordered(part, axis, bits):
    wide = part.shape[-1] // 2
    first = part[..., :wide][None]
    first = ordered(bits[0], first, swap(first, axis, 1))
    first = ordered(bits[1], first, swap(first, axis, 3))
    second = part[..., wide:][None]
    second = ordered(bits[1], second, swap(second, axis, 3))
    theirs = swap(second, axis, 1)
    kind = bits[0] ^ bits[1]
    outer = jnp.where(kind == 0, second, theirs)
    inner = jnp.where(kind == 0, theirs, second)
    second = jnp.concatenate([outer[:1], inner, outer[1:]], axis=0)
    return jnp.concatenate([first, second], axis=-1)


def silu_grad(values_in):
    sigmoid_of = jax.nn.sigmoid(values_in)
    return sigmoid_of * (1.0 + values_in * (1.0 - sigmoid_of))


def slot_tables(route_rows, gate_rows):
    tokens = route_rows.shape[0]
    experts = jnp.arange(EXPERTS, dtype=jnp.int32)
    same = route_rows.T[None, :, :] == experts[:, None, None]
    hits = jnp.sum(same.astype(F32), axis=1)
    gates = jnp.sum(jnp.where(same, gate_rows.T[None, :, :], 0.0), axis=1)
    token_iota = jnp.arange(tokens, dtype=jnp.int32)
    earlier = (token_iota[:, None] < token_iota[None, :]).astype(BF16)
    rank = jnp.dot(hits.astype(BF16), earlier, preferred_element_type=F32)
    places = jnp.arange(CAP, dtype=jnp.int32).astype(F32)
    picked = (rank[:, None, :] == places[None, :, None]) & (hits[:, None, :] > 0.5)
    picker = picked.astype(F32).reshape(EXPERTS * CAP, tokens)
    weigher = jnp.where(picked, gates[:, None, :], 0.0).reshape(EXPERTS * CAP, tokens)
    return picker, weigher


def dispatched(slots, col_blocks):
    wide = slots.shape[1] // col_blocks
    pieces = slots.reshape(EXPERTS, CAP, col_blocks, wide).transpose(2, 0, 1, 3)
    pieces = pieces.reshape(col_blocks * EXPERTS, CAP, wide)
    pieces = lax.all_to_all(pieces, ("zh", "y") + EXP, split_axis=0, concat_axis=0, tiled=True)
    return pieces.reshape(col_blocks * EXPERTS * CAP, wide)


def returned(rows, col_blocks):
    wide = rows.shape[1]
    pieces = rows.reshape(col_blocks * EXPERTS, CAP, wide)
    pieces = lax.all_to_all(pieces, ("zh", "y") + EXP, split_axis=0, concat_axis=0, tiled=True)
    pieces = pieces.reshape(col_blocks, EXPERTS, CAP, wide).transpose(1, 2, 0, 3)
    return pieces.reshape(EXPERTS * CAP, col_blocks * wide)


def shards(
    residual,
    queries,
    latent,
    out_proj,
    up_weight,
    down_weight,
    cotangent,
    routes,
    gate_values,
    documents,
):
    zh = lax.axis_index("zh")
    y = lax.axis_index("y")
    core = lax.axis_index("core")
    x = lax.axis_index("x")
    y_bits = (y & 1, y >> 1)
    tokens = residual.shape[1]
    model_width = residual.shape[2]
    col_blocks = 8
    wide = model_width // col_blocks
    inv_root = 1.0 / math.sqrt(LAT)

    own = latent[0]
    before = lax.ppermute(own, "zh", [(0, 1)])
    both = gather_relative(jnp.stack([own, before]), "y")
    y_xors = jnp.array([0, 1, 3, 2], jnp.int32)
    blocks_y = y ^ y_xors
    place = 2 * y + core
    held_place = 2 * blocks_y + core
    mine = jnp.where((held_place <= place)[:, None, None], both[:, 0], both[:, 1])
    for_partner = jnp.where(
        (held_place <= 2 * y + (1 - core))[:, None, None], both[:, 0], both[:, 1]
    )
    theirs = swap(for_partner, "core", 1)
    keys = jnp.concatenate([mine, theirs], axis=0)
    keys = keys.reshape(8 * tokens, LAT)
    places = jnp.concatenate([held_place, 2 * blocks_y + (1 - core)])
    blocks = jnp.where(places <= place, zh * 8 + places, (zh - 1) * 8 + places)
    doc_row = documents[0]
    block_iota = jnp.arange(doc_row.shape[0], dtype=jnp.int32)
    block_docs = jnp.sum(
        jnp.where(blocks[:, None] == block_iota[None, :], doc_row[None, :], 0), axis=1
    )
    my_block = zh * 8 + place
    my_doc = jnp.sum(jnp.where(block_iota == my_block, doc_row, 0))
    block_open = (block_docs == my_doc) & (blocks >= 0) & (blocks <= my_block)
    token_iota = jnp.arange(tokens, dtype=jnp.int32)
    key_limit = jnp.where(
        block_open[:, None],
        jnp.where((blocks == my_block)[:, None], token_iota[None, :], -1),
        tokens,
    ).reshape(1, 8 * tokens)
    query_rows = jnp.concatenate([queries[0][:, :LAT], queries[0][:, LAT:]], axis=0)
    allowed = key_limit <= jnp.concatenate([token_iota, token_iota])[:, None]
    scores = (
        lax.dot_general(query_rows, keys, (((1,), (1,)), ((), ())), preferred_element_type=F32)
        * inv_root
    )
    scores = jnp.where(allowed, scores, -1e30)
    largest = jnp.max(scores, axis=1, keepdims=True)
    exponent = jnp.where(allowed, jnp.exp(scores - largest), 0.0)
    total = jnp.sum(exponent, axis=1, keepdims=True)
    mixed = jnp.dot(exponent.astype(BF16), keys, preferred_element_type=F32) / total
    mixed = mixed.astype(BF16)
    heads_out = jnp.concatenate([mixed[:tokens], mixed[tokens:]], axis=1)

    picker, weigher = slot_tables(routes[0], gate_values[0])
    picker_half = picker.astype(BF16)
    slot_gate = jnp.sum(weigher, axis=1)
    slot_cot = (
        jnp.dot(picker_half, cotangent[0], preferred_element_type=F32) * slot_gate[:, None]
    ).astype(BF16)
    slot_res = jnp.dot(picker_half, residual[0], preferred_element_type=F32).astype(BF16)
    cot_rows = dispatched(slot_cot, col_blocks)
    res_rows = dispatched(slot_res, col_blocks)

    chip_axes = ("zh", "y")
    cols_rows = out_proj.reshape(-1, col_blocks, wide).transpose(1, 0, 2)
    cols_rows = lax.all_to_all(cols_rows, chip_axes, split_axis=0, concat_axis=0, tiled=True)
    theirs = swap(cols_rows, "core", 1)
    chip_cols = ordered(core, cols_rows[:, None], theirs[:, None], 1).reshape(-1, wide)

    slot_heads = jnp.dot(picker_half, heads_out, preferred_element_type=F32).astype(BF16)
    heads_rows_own = lax.all_to_all(
        slot_heads.reshape(EXPERTS, CAP, -1), EXP, split_axis=0, concat_axis=0, tiled=True
    ).reshape(EXPERTS * CAP, HEADS * LAT)
    heads_rows = gather_ordered(heads_rows_own, "y", y_bits).reshape(-1, HEADS * LAT)
    heads_rows = ordered(zh, heads_rows, swap(heads_rows, "zh", 1))
    in_rows = (
        res_rows.astype(F32) + jnp.dot(heads_rows, chip_cols, preferred_element_type=F32)
    ).astype(BF16)

    my_cols = 4 * core + x
    mine = lax.dynamic_slice_in_dim(out_proj, my_cols * wide, wide, 1)
    theirs = lax.dynamic_slice_in_dim(out_proj, (my_cols ^ 4) * wide, wide, 1)
    theirs = swap(theirs, "core", 1)
    proj_block = lax.all_gather(ordered(core, mine, theirs), chip_axes, axis=0, tiled=True)
    group_rows = lax.all_gather(heads_out, ("core", "x"), axis=0, tiled=True)
    projected = jnp.dot(group_rows, proj_block, preferred_element_type=F32).astype(BF16)
    projected = projected.reshape(8, tokens, wide)
    projected = lax.all_to_all(projected, ("core", "x"), split_axis=0, concat_axis=0, tiled=True)
    projected = lax.optimization_barrier(projected.transpose(1, 0, 2).reshape(tokens, -1))
    hidden_in = (residual[0].astype(F32) + projected.astype(F32)).astype(BF16)

    up_own, down_own = up_weight[0], down_weight[0]
    up_part = ordered(core, up_own, swap(up_own, "core", 1))
    down_part = ordered(core, down_own, swap(down_own, "core", 1), 1)
    contract_rows = (((0,), (0,)), ((), ()))
    contract_cols = (((1,), (1,)), ((), ()))
    grad_part = lax.dot_general(cot_rows, down_part, contract_cols, preferred_element_type=F32)
    sum_bits = (y_bits[0] ^ y_bits[1], y_bits[1])
    grad_full = lax.psum(grad_part.astype(BF16), chip_axes).astype(F32)
    pre_part = jnp.dot(in_rows, up_part, preferred_element_type=F32)
    pre_full = sum_chips(pre_part.astype(BF16), sum_bits).astype(F32)
    activated = jax.nn.silu(pre_full).astype(BF16)
    pre_grad = (grad_full * silu_grad(pre_full)).astype(BF16)
    slot_out = jnp.dot(activated, down_part, preferred_element_type=F32).astype(BF16)
    back_out = returned(slot_out, col_blocks)
    slot_in_grad = lax.dot_general(
        pre_grad, up_part, contract_cols, preferred_element_type=F32
    ).astype(BF16)
    back_grad = returned(slot_in_grad, col_blocks)

    down_both = lax.dot_general(activated, cot_rows, contract_rows, preferred_element_type=F32)
    part_width = wide // 2
    low, high = down_both[:, :part_width], down_both[:, part_width:]
    down_mine = jnp.where(core == 0, low, high)
    down_theirs = jnp.where(core == 0, high, low).astype(BF16)
    down_grad = (down_mine + swap(down_theirs, "core", 1).astype(F32)).astype(BF16)
    up_both = lax.dot_general(in_rows, pre_grad, contract_rows, preferred_element_type=F32)
    up_mine = half_of(up_both, core)
    up_theirs = half_of(up_both, 1 - core).astype(BF16)
    up_grad = (up_mine + swap(up_theirs, "core", 1).astype(F32)).astype(BF16)

    gate_high = weigher.astype(BF16)
    gate_low = (weigher - gate_high.astype(F32)).astype(BF16)
    gathered_out = lax.dot_general(
        jnp.concatenate([gate_high, gate_low], axis=0),
        jnp.concatenate([back_out, back_out], axis=0),
        contract_rows,
        preferred_element_type=F32,
    )
    gathered_grad = lax.dot_general(
        picker_half, back_grad, contract_rows, preferred_element_type=F32
    )
    layer_out = (hidden_in.astype(F32) + gathered_out).astype(BF16)
    input_grad = (cotangent[0].astype(F32) + gathered_grad).astype(BF16)
    return (layer_out[None], input_grad[None], up_grad[None], down_grad[None])


def solution(mesh):
    grid = Mesh(mesh.devices.reshape(2, 4, 2, 4, 4), CTX + EXP)
    placed = (
        P(EXP, CTX, None),
        P(EXP, CTX, None),
        P(EXP, CTX, None),
        P(CTX, None),
        P(EXP, CTX, None),
        P(EXP, None, CTX),
        P(EXP, CTX, None),
        P(EXP, CTX, None),
        P(EXP, CTX, None),
        P(EXP, None),
    )

    return jax.shard_map(
        shards,
        mesh=grid,
        in_specs=placed,
        out_specs=(
            P(EXP, CTX, None),
            P(EXP, CTX, None),
            P(EXP, CTX, None),
            P(EXP, None, CTX),
        ),
        check_vma=False,
    )
```

```python
import math

import jax
import jax.numpy as jnp
from jax import lax
from jax.sharding import Mesh
from jax.sharding import PartitionSpec as P


LAT = 512
HEADS = 2
CAP = 4
EXPERTS = 16
CTX = ("zh", "y", "core")
EXP = ("zl", "x")
F32 = jnp.float32
BF16 = jnp.bfloat16


def swap(part, axis, mask):
    peers = lax.axis_size(axis)
    return lax.ppermute(part, axis, [(i, i ^ mask) for i in range(peers)])


def ordered(bit, mine, theirs, dim=0):
    low = jnp.where(bit == 0, mine, theirs)
    high = jnp.where(bit == 0, theirs, mine)
    return jnp.concatenate([low, high], axis=dim)


def add_rounded(a, b):
    return (a.astype(F32) + b.astype(F32)).astype(BF16)


def half_of(part, bit):
    rows = part.shape[0] // 2
    return lax.dynamic_slice_in_dim(part, bit * rows, rows, 0)


def sum_chips(parts, bits):
    orders = (((1, bits[0]), (3, bits[1])), ((3, bits[1]), (1, bits[0])))
    reduced = []
    for held, order in zip(parts, orders):
        for mask, bit in order:
            held = add_rounded(half_of(held, bit), swap(half_of(held, 1 - bit), "y", mask))
        reduced.append(held)
    reduced = [add_rounded(h, swap(h, "zh", 1)) for h in reduced]
    full = []
    for held, order in zip(reduced, orders):
        for mask, bit in reversed(order):
            held = ordered(bit, held, swap(held, "y", mask))
        full.append(held)
    return full


def gather_relative(part, axis):
    wide = part.shape[-1] // 2
    halves = []
    for half, masks in enumerate(((1, 3), (3, 1))):
        held = part[..., half * wide : (half + 1) * wide][None]
        for mask in masks:
            held = jnp.concatenate([held, swap(held, axis, mask)], axis=0)
        if half == 1:
            held = jnp.stack([held[0], held[2], held[1], held[3]], axis=0)
        halves.append(held)
    return jnp.concatenate(halves, axis=-1)


def gather_ordered(part, axis, bits):
    wide = part.shape[-1] // 2
    first = part[..., :wide][None]
    first = ordered(bits[0], first, swap(first, axis, 1))
    first = ordered(bits[1], first, swap(first, axis, 3))
    second = part[..., wide:][None]
    second = ordered(bits[1], second, swap(second, axis, 3))
    theirs = swap(second, axis, 1)
    kind = bits[0] ^ bits[1]
    outer = jnp.where(kind == 0, second, theirs)
    inner = jnp.where(kind == 0, theirs, second)
    second = jnp.concatenate([outer[:1], inner, outer[1:]], axis=0)
    return jnp.concatenate([first, second], axis=-1)


def mirror_z(part):
    return lax.ppermute(part, ("zh", "zl"), [(i, 7 - i) for i in range(8)])


def by_source(pieces, bits):
    for place, bit in enumerate(bits):
        pieces = [
            jnp.where(bit == 0, pieces[m], pieces[m ^ (1 << place)]) for m in range(len(pieces))
        ]
    return jnp.stack(pieces)


def col_piece(part, index, wide):
    return lax.dynamic_slice_in_dim(part, index * wide, wide, part.ndim - 1)


def silu_grad(values_in):
    sigmoid_of = jax.nn.sigmoid(values_in)
    return sigmoid_of * (1.0 + values_in * (1.0 - sigmoid_of))


def slot_tables(route_rows, gate_rows):
    tokens = route_rows.shape[0]
    experts = jnp.arange(EXPERTS, dtype=jnp.int32)
    same = route_rows.T[None, :, :] == experts[:, None, None]
    hits = jnp.sum(same.astype(F32), axis=1)
    gates = jnp.sum(jnp.where(same, gate_rows.T[None, :, :], 0.0), axis=1)
    token_iota = jnp.arange(tokens, dtype=jnp.int32)
    earlier = (token_iota[:, None] < token_iota[None, :]).astype(BF16)
    rank = jnp.dot(hits.astype(BF16), earlier, preferred_element_type=F32)
    places = jnp.arange(CAP, dtype=jnp.int32).astype(F32)
    picked = (rank[:, None, :] == places[None, :, None]) & (hits[:, None, :] > 0.5)
    picker = picked.astype(F32).reshape(EXPERTS * CAP, tokens)
    weigher = jnp.where(picked, gates[:, None, :], 0.0).reshape(EXPERTS * CAP, tokens)
    return picker, weigher


def dispatched(slots, col_blocks):
    wide = slots.shape[1] // col_blocks
    pieces = slots.reshape(EXPERTS, CAP, col_blocks, wide).transpose(2, 0, 1, 3)
    pieces = pieces.reshape(col_blocks * EXPERTS, CAP, wide)
    pieces = lax.all_to_all(pieces, ("zh", "y") + EXP, split_axis=0, concat_axis=0, tiled=True)
    return pieces.reshape(col_blocks * EXPERTS * CAP, wide)


def returned(rows, col_blocks):
    wide = rows.shape[1]
    pieces = rows.reshape(col_blocks * EXPERTS, CAP, wide)
    pieces = lax.all_to_all(pieces, ("zh", "y") + EXP, split_axis=0, concat_axis=0, tiled=True)
    pieces = pieces.reshape(col_blocks, EXPERTS, CAP, wide).transpose(1, 2, 0, 3)
    return pieces.reshape(EXPERTS * CAP, col_blocks * wide)


def shards(
    residual,
    queries,
    latent,
    out_proj,
    up_weight,
    down_weight,
    cotangent,
    routes,
    gate_values,
    documents,
):
    zh = lax.axis_index("zh")
    y = lax.axis_index("y")
    core = lax.axis_index("core")
    x = lax.axis_index("x")
    y_bits = (y & 1, y >> 1)
    tokens = residual.shape[1]
    model_width = residual.shape[2]
    col_blocks = 8
    wide = model_width // col_blocks
    inv_root = 1.0 / math.sqrt(LAT)

    own = latent[0]
    before = lax.ppermute(own, "zh", [(0, 1)])
    both = gather_relative(jnp.stack([own, before]), "y")
    y_xors = jnp.array([0, 1, 3, 2], jnp.int32)
    blocks_y = y ^ y_xors
    place = 2 * y + core
    held_place = 2 * blocks_y + core
    mine = jnp.where((held_place <= place)[:, None, None], both[:, 0], both[:, 1])
    for_partner = jnp.where(
        (held_place <= 2 * y + (1 - core))[:, None, None], both[:, 0], both[:, 1]
    )
    theirs = swap(for_partner, "core", 1)
    keys = jnp.concatenate([mine, theirs], axis=0)
    keys = keys.reshape(8 * tokens, LAT)
    places = jnp.concatenate([held_place, 2 * blocks_y + (1 - core)])
    blocks = jnp.where(places <= place, zh * 8 + places, (zh - 1) * 8 + places)
    doc_row = documents[0]
    block_iota = jnp.arange(doc_row.shape[0], dtype=jnp.int32)
    block_docs = jnp.sum(
        jnp.where(blocks[:, None] == block_iota[None, :], doc_row[None, :], 0), axis=1
    )
    my_block = zh * 8 + place
    my_doc = jnp.sum(jnp.where(block_iota == my_block, doc_row, 0))
    block_open = (block_docs == my_doc) & (blocks >= 0) & (blocks <= my_block)
    token_iota = jnp.arange(tokens, dtype=jnp.int32)
    key_limit = jnp.where(
        block_open[:, None],
        jnp.where((blocks == my_block)[:, None], token_iota[None, :], -1),
        tokens,
    ).reshape(1, 8 * tokens)
    query_rows = jnp.concatenate([queries[0][:, :LAT], queries[0][:, LAT:]], axis=0)
    allowed = key_limit <= jnp.concatenate([token_iota, token_iota])[:, None]
    scores = (
        lax.dot_general(query_rows, keys, (((1,), (1,)), ((), ())), preferred_element_type=F32)
        * inv_root
    )
    scores = jnp.where(allowed, scores, -1e30)
    largest = jnp.max(scores, axis=1, keepdims=True)
    exponent = jnp.where(allowed, jnp.exp(scores - largest), 0.0)
    total = jnp.sum(exponent, axis=1, keepdims=True)
    mixed = jnp.dot(exponent.astype(BF16), keys, preferred_element_type=F32) / total
    mixed = mixed.astype(BF16)
    heads_out = jnp.concatenate([mixed[:tokens], mixed[tokens:]], axis=1)

    picker, weigher = slot_tables(routes[0], gate_values[0])
    picker_half = picker.astype(BF16)
    slot_gate = jnp.sum(weigher, axis=1)
    slot_cot = (
        jnp.dot(picker_half, cotangent[0], preferred_element_type=F32) * slot_gate[:, None]
    ).astype(BF16)
    slot_res = jnp.dot(picker_half, residual[0], preferred_element_type=F32).astype(BF16)
    cot_rows = dispatched(slot_cot, col_blocks)
    res_rows = dispatched(slot_res, col_blocks)

    chip_axes = ("zh", "y")
    half_width = model_width // 2
    cols_mine = lax.dynamic_slice_in_dim(out_proj, zh * half_width, half_width, 1)
    cols_other = lax.dynamic_slice_in_dim(out_proj, (1 - zh) * half_width, half_width, 1)
    half_rows = ordered(zh, cols_mine[None], mirror_z(cols_other)[None])
    pieces = [col_piece(half_rows, y, wide)]
    for mask in (1, 2, 3):
        pieces.append(swap(col_piece(half_rows, y ^ mask, wide), "y", mask))
    by_y = by_source(pieces, y_bits)
    by_core = ordered(core, by_y[None], swap(by_y, "core", 1)[None])
    chip_cols = by_core.transpose(2, 1, 0, 3, 4).reshape(HEADS * LAT, wide)

    slot_heads = jnp.dot(picker_half, heads_out, preferred_element_type=F32).astype(BF16)
    heads_rows_own = lax.all_to_all(
        slot_heads.reshape(EXPERTS, CAP, -1), EXP, split_axis=0, concat_axis=0, tiled=True
    ).reshape(EXPERTS * CAP, HEADS * LAT)
    heads_rows = gather_ordered(heads_rows_own, "y", y_bits).reshape(-1, HEADS * LAT)
    heads_rows = ordered(zh, heads_rows, swap(heads_rows, "zh", 1))
    in_rows = (
        res_rows.astype(F32) + jnp.dot(heads_rows, chip_cols, preferred_element_type=F32)
    ).astype(BF16)

    my_cols = 4 * core + x
    mine = lax.dynamic_slice_in_dim(out_proj, my_cols * wide, wide, 1)
    theirs = lax.dynamic_slice_in_dim(out_proj, (my_cols ^ 4) * wide, wide, 1)
    theirs = swap(theirs, "core", 1)
    proj_block = lax.all_gather(ordered(core, mine, theirs), chip_axes, axis=0, tiled=True)
    group_rows = lax.all_gather(heads_out, ("core", "x"), axis=0, tiled=True)
    projected = jnp.dot(group_rows, proj_block, preferred_element_type=F32).astype(BF16)
    projected = projected.reshape(8, tokens, wide)
    projected = lax.all_to_all(projected, ("core", "x"), split_axis=0, concat_axis=0, tiled=True)
    projected = lax.optimization_barrier(projected.transpose(1, 0, 2).reshape(tokens, -1))
    hidden_in = (residual[0].astype(F32) + projected.astype(F32)).astype(BF16)

    up_own, down_own = up_weight[0], down_weight[0]
    up_part = ordered(core, up_own, swap(up_own, "core", 1))
    down_part = ordered(core, down_own, swap(down_own, "core", 1), 1)
    contract_rows = (((0,), (0,)), ((), ()))
    contract_cols = (((1,), (1,)), ((), ()))
    grad_part = lax.dot_general(cot_rows, down_part, contract_cols, preferred_element_type=F32)
    sum_bits = (y_bits[0] ^ y_bits[1], y_bits[1])
    pre_part = jnp.dot(in_rows, up_part, preferred_element_type=F32)
    sums = sum_chips((pre_part.astype(BF16), grad_part.astype(BF16)), sum_bits)
    pre_full, grad_full = sums[0].astype(F32), sums[1].astype(F32)
    activated = jax.nn.silu(pre_full).astype(BF16)
    pre_grad = (grad_full * silu_grad(pre_full)).astype(BF16)
    slot_out = jnp.dot(activated, down_part, preferred_element_type=F32).astype(BF16)
    back_out = returned(slot_out, col_blocks)
    slot_in_grad = lax.dot_general(
        pre_grad, up_part, contract_cols, preferred_element_type=F32
    ).astype(BF16)
    back_grad = returned(slot_in_grad, col_blocks)

    down_both = lax.dot_general(activated, cot_rows, contract_rows, preferred_element_type=F32)
    part_width = wide // 2
    low, high = down_both[:, :part_width], down_both[:, part_width:]
    down_mine = jnp.where(core == 0, low, high)
    down_theirs = jnp.where(core == 0, high, low).astype(BF16)
    down_grad = (down_mine + swap(down_theirs, "core", 1).astype(F32)).astype(BF16)
    up_both = lax.dot_general(in_rows, pre_grad, contract_rows, preferred_element_type=F32)
    up_mine = half_of(up_both, core)
    up_theirs = half_of(up_both, 1 - core).astype(BF16)
    up_grad = (up_mine + swap(up_theirs, "core", 1).astype(F32)).astype(BF16)

    gate_high = weigher.astype(BF16)
    gate_low = (weigher - gate_high.astype(F32)).astype(BF16)
    gathered_out = lax.dot_general(
        jnp.concatenate([gate_high, gate_low], axis=0),
        jnp.concatenate([back_out, back_out], axis=0),
        contract_rows,
        preferred_element_type=F32,
    )
    gathered_grad = lax.dot_general(
        picker_half, back_grad, contract_rows, preferred_element_type=F32
    )
    layer_out = (hidden_in.astype(F32) + gathered_out).astype(BF16)
    input_grad = (cotangent[0].astype(F32) + gathered_grad).astype(BF16)
    return (layer_out[None], input_grad[None], up_grad[None], down_grad[None])


def solution(mesh):
    grid = Mesh(mesh.devices.reshape(2, 4, 2, 4, 4), CTX + EXP)
    placed = (
        P(EXP, CTX, None),
        P(EXP, CTX, None),
        P(EXP, CTX, None),
        P(CTX, None),
        P(EXP, CTX, None),
        P(EXP, None, CTX),
        P(EXP, CTX, None),
        P(EXP, CTX, None),
        P(EXP, CTX, None),
        P(EXP, None),
    )

    return jax.shard_map(
        shards,
        mesh=grid,
        in_specs=placed,
        out_specs=(
            P(EXP, CTX, None),
            P(EXP, CTX, None),
            P(EXP, CTX, None),
            P(EXP, None, CTX),
        ),
        check_vma=False,
    )
```
